32 devices in a mesh: dp: 2 (over x), row: 4 (over z), col: 4 (over y, core).
Axes of the slice: x: 2, y: 2, z: 4, core: 2. Of those that a mesh axis runs over, the one named last changes fastest.
Arguments:
- tokens: bfloat16 [4, 2048, 2048], P('dp', 'row', 'col'), may hold values from -6 to 6
- lengths: int32 [4], P('dp'), may hold values from 682 to 2048, as said below
- cotangent: bfloat16 [4, 2048, 2048], P('dp', 'row', 'col'), may hold values from -6 to 6
- norm1_gain: float32 [2048], P('col'), may hold values from 0.25 to 1.75
- norm1_bias: float32 [2048], P('col'), may hold values from -3 to 3
- query_weight: bfloat16 [2048, 2048], P('col', 'row'), may hold values from -0.125 to 0.125
- kv_weight: bfloat16 [2048, 256], P('col'), may hold values from -0.125 to 0.125
- out_weight: bfloat16 [2048, 2048], P('row', 'col'), may hold values from -1 to 1
- norm2_gain: float32 [2048], P('col'), may hold values from 0.25 to 1.75
- norm2_bias: float32 [2048], P('col'), may hold values from -3 to 3
- up_weight: bfloat16 [2048, 8192], P('col', 'row'), may hold values from -0.125 to 0.125
- down_weight: bfloat16 [8192, 2048], P('row', 'col'), may hold values from -0.0625 to 0.0625
Outputs:
- out: bfloat16 [4, 2048, 2048], P('dp', 'row', 'col')
- grad_input: bfloat16 [4, 2048, 2048], P('dp', 'row', 'col')
- grad_norm1_gain: float32 [2048], P('col')
- grad_norm1_bias: float32 [2048], P('col')
- grad_query_weight: float32 [2048, 2048], P('col', 'row')
- grad_kv_weight: float32 [2048, 256], P('col')
- grad_out_weight: float32 [2048, 2048], P('row', 'col')
- grad_norm2_gain: float32 [2048], P('col')
- grad_norm2_bias: float32 [2048], P('col')
- grad_up_weight: float32 [2048, 8192], P('col', 'row')
- grad_down_weight: float32 [8192, 2048], P('row', 'col')
The draws below stay inside these ranges and needn't reach their ends.
Inputs may be any that keep to these rules, and one draw needn't show every extreme that they name: `lengths`: entry s is the number of valid slots of sequence s; sequences s * 2 to s * 2 + 1 belong to index s of dp. Some sequence has all 2048 slots valid.
All inputs are finite; a program needn't handle non-finite values.
Results may differ from the reference program's by a relative error of at most 0.02.
Values may be sent and summed in bfloat16 or wider, within the bound.
A program may use at most 256 MiB of HBM per device.

```python
from functools import partial
import jax
import jax.numpy as jnp
from jax import lax

D = 2048
HEADS = 16
HEAD_DIM = 128
FF = 8192
SLOTS = 2048
SEQS = 4


def draw_lengths(key, part):
    lengths = jax.random.randint(jax.random.fold_in(key, 11), (SEQS,), SLOTS // 3, SLOTS + 1)
    full_seq = jax.random.randint(jax.random.fold_in(key, 12), (), 0, SEQS)
    return jnp.where(jnp.arange(SEQS) == full_seq, SLOTS, lengths).astype(jnp.int32)


def levels(rng, dims, cuts, smallest, high):
    def one(position, blocks):
        draws = jax.random.uniform(jax.random.fold_in(jax.random.fold_in(rng, 6), position), (blocks,), jnp.float32, smallest / len(cuts), high / len(cuts))
        return jnp.repeat(jnp.exp(draws), dims[position] // blocks).reshape((-1,) + (1,) * (len(dims) - position - 1))

    gain = one(*cuts[0])
    for cut in cuts[1:]:
        gain = gain * one(*cut)
    return gain


def normal_values(rng, dims, deviation, reach, shards=(), kind=jnp.bfloat16):
    entries = deviation * jax.random.normal(rng, dims, jnp.float32)
    if shards:
        entries = entries * levels(rng, dims, shards, -0.22, 0.18)
    return jnp.clip(entries, -reach, reach).astype(kind)


def setup_inputs(seed: int = 0) -> dict:
    key_list = jax.random.split(jax.random.key(seed), 13)
    return {
        "tokens": normal_values(key_list[0], (SEQS, SLOTS, D), 1.0, 6.0, ((0, 2), (1, 4), (2, 4))),
        "lengths": draw_lengths(jax.random.fold_in(key_list[12], 71), 0),
        "cotangent": normal_values(key_list[2], (SEQS, SLOTS, D), 1.0, 6.0, ((0, 2), (1, 4), (2, 4))),
        "norm1_gain": jnp.clip(1.0 + 0.15 * jax.random.normal(key_list[3], (D,), jnp.float32), 0.25, 1.75),
        "norm1_bias": normal_values(key_list[4], (D,), 0.5, 3.0, ((0, 4),), jnp.float32),
        "query_weight": normal_values(key_list[5], (D, HEADS * HEAD_DIM), D ** -0.5, 0.125, ((0, 4), (1, 4))),
        "kv_weight": normal_values(key_list[6], (D, 2 * HEAD_DIM), D ** -0.5, 0.125, ((0, 4),)),
        "out_weight": normal_values(key_list[7], (HEADS * HEAD_DIM, D), (max(D // 64, 4)) ** -0.5, 1.0, ((0, 4), (1, 4))),
        "norm2_gain": jnp.clip(1.0 + 0.15 * jax.random.normal(key_list[8], (D,), jnp.float32), 0.25, 1.75),
        "norm2_bias": normal_values(key_list[9], (D,), 0.5, 3.0, ((0, 4),), jnp.float32),
        "up_weight": normal_values(key_list[10], (D, FF), D ** -0.5, 0.125, ((0, 4), (1, 4))),
        "down_weight": normal_values(key_list[11], (FF, D), FF ** -0.5, 0.0625, ((0, 4), (1, 4))),
    }


eps = 1e-05

@jax.custom_vjp
def low(v):
    return lax.optimization_barrier(v.astype(jnp.bfloat16)).astype(jnp.float32)

@jax.custom_vjp
def low_back(v):
    return v

def low_keep(v):
    return (low(v), None)

def low_pass(kept, grad):
    return (grad,)

def back_keep(v):
    return (v, None)

def back_low(kept, grad):
    return (low(grad),)
low.defvjp(low_keep, low_pass)
low_back.defvjp(back_keep, back_low)

def matmul(left_side, right_side):
    return jnp.dot(left_side, right_side, precision=lax.Precision.HIGHEST, preferred_element_type=jnp.float32)

def layer_norm(hidden, norm_gain, norm_bias, row_keep):
    centre = lax.optimization_barrier(jnp.mean(hidden, axis=1, keepdims=True))
    spread = lax.optimization_barrier(jnp.mean(hidden * hidden, axis=1, keepdims=True)) - centre * centre
    normed = (hidden - centre) * lax.rsqrt(spread + eps)
    return row_keep * (normed * norm_gain + norm_bias)

def one_head(key_rows, value_rows, allowed, query_head):
    scaling = query_head.shape[1] ** (-0.5)
    scores = low_back(matmul(query_head, key_rows.T) * scaling)
    scores = jnp.where(allowed, scores, -jnp.inf)
    log_total = jax.nn.logsumexp(scores, axis=1, keepdims=True)
    weights = low(jnp.exp(scores - log_total))
    return matmul(weights, value_rows)

def sequence_forward(seq_tokens, params, seq_length):
    norm1_gain, norm1_bias, query_weight, kv_weight, out_weight, norm2_gain, norm2_bias, up_weight, down_weight = params
    slot_count = seq_tokens.shape[0]
    positions = jnp.arange(slot_count, dtype=jnp.int32)
    row_keep = (positions < seq_length).astype(jnp.float32)[:, None]
    allowed = (positions[None, :] <= positions[:, None]) & (positions[None, :] < seq_length)
    norm_one = low(layer_norm(seq_tokens, norm1_gain, norm1_bias, row_keep))
    queries = low(low_back(matmul(norm_one, query_weight)))
    key_value = low(low_back(matmul(norm_one, kv_weight)))
    head_size = key_value.shape[1] // 2
    head_count = queries.shape[1] // head_size
    stacked = queries.reshape(slot_count, head_count, head_size).transpose(1, 0, 2)
    head_fn = jax.checkpoint(partial(one_head, key_value[:, :head_size], key_value[:, head_size:], allowed))
    per_head = lax.map(head_fn, stacked)
    attended = low(low_back(per_head.transpose(1, 0, 2).reshape(slot_count, head_count * head_size)))
    middle = seq_tokens + low_back(matmul(attended, out_weight))
    norm_two = low(layer_norm(middle, norm2_gain, norm2_bias, row_keep))
    up_sums = low_back(matmul(norm_two, up_weight))
    activated = low(jax.nn.gelu(up_sums, approximate=True))
    return row_keep * (middle + low_back(matmul(activated, down_weight)))

def reference(tokens, lengths, cotangent, norm1_gain, norm1_bias, query_weight, kv_weight, out_weight, norm2_gain, norm2_bias, up_weight, down_weight):
    params = tuple((weight_array.astype(jnp.float32) for weight_array in (norm1_gain, norm1_bias, query_weight, kv_weight, out_weight, norm2_gain, norm2_bias, up_weight, down_weight)))

    def sequence_step(totals, packed):
        seq_tokens, seq_cotangent, seq_length = packed
        result, pullback = jax.vjp(partial(sequence_forward, seq_length=seq_length), seq_tokens.astype(jnp.float32), params)
        grad_tokens, grad_params = pullback(seq_cotangent.astype(jnp.float32))
        totals = tuple((total_term + new_term for total_term, new_term in zip(totals, grad_params)))
        return (totals, (result.astype(jnp.bfloat16), grad_tokens.astype(jnp.bfloat16)))
    start_totals = tuple((jnp.zeros(weight_array.shape, jnp.float32) for weight_array in params))
    totals, (outputs, grad_inputs) = lax.scan(sequence_step, start_totals, (tokens, cotangent, lengths))
    return (outputs, grad_inputs, totals[0], totals[1], totals[2], totals[3], totals[4], totals[5], totals[6], totals[7], totals[8])
```

```python
import jax
import jax.numpy as jnp
from jax import lax
from jax.sharding import PartitionSpec as P

eps = 1e-05
BF = jnp.bfloat16
F32 = jnp.float32


def mm(a, b, ca, cb):
    return lax.dot_general(a, b, (((ca,), (cb,)), ((), ())), preferred_element_type=F32)


def norm_stats(hidden):
    centre = jnp.mean(hidden, axis=1, keepdims=True)
    spread = jnp.mean(hidden * hidden, axis=1, keepdims=True) - centre * centre
    return centre, lax.rsqrt(spread + eps)


def norm_apply(hidden, centre, inverse, gain, bias, keep):
    return (keep * ((hidden - centre) * inverse * gain + bias)).astype(BF)


def norm_backward(gradient, normed, inverse, gain, keep):
    masked = keep * gradient
    scaled = masked * gain
    first = jnp.mean(scaled, axis=1, keepdims=True)
    second = jnp.mean(scaled * normed, axis=1, keepdims=True)
    result = inverse * (scaled - first - normed * second)
    return result, jnp.sum(masked * normed, axis=0), jnp.sum(masked, axis=0)


def turn(weight):
    return lax.all_to_all(weight, "col", 0, 1, tiled=True)


def turn_back(rows):
    return lax.all_to_all(rows, "col", 1, 0, tiled=True)


def gather(x, axes, dim=0):
    return lax.all_gather(x, axes, axis=dim, tiled=True)


def scatter(x, axes):
    return lax.psum_scatter(x, axes, scatter_dimension=0, tiled=True)


def pairs_allowed(first, count, keys, length):
    q = first + jnp.arange(count, dtype=jnp.int32)[:, None]
    k = jnp.arange(keys, dtype=jnp.int32)[None, :]
    return (k <= q) & (k < length)


def attend(queries, kv, lengths, first):
    b, t, width = queries.shape
    hd = kv.shape[2] // 2
    outs, logs = [], []
    for s in range(b):
        keys, values = kv[s, :, :hd], kv[s, :, hd:]
        allowed = pairs_allowed(first, t, kv.shape[1], lengths[s])
        for h in range(width // hd):
            q = queries[s, :, h * hd : (h + 1) * hd]
            scores = jnp.where(allowed, mm(q, keys, 1, 1) * hd**-0.5, -jnp.inf)
            top = jnp.max(scores, axis=1, keepdims=True)
            log_total = top + jnp.log(jnp.sum(jnp.exp(scores - top), axis=1, keepdims=True))
            weights = jnp.exp(scores - log_total).astype(BF)
            outs.append(mm(weights, values, 1, 0).astype(BF))
            logs.append(log_total)
    n = width // hd
    out = jnp.stack([jnp.concatenate(outs[s * n : (s + 1) * n], axis=1) for s in range(b)])
    log = jnp.stack([jnp.concatenate(logs[s * n : (s + 1) * n], axis=1) for s in range(b)])
    return out, log


def attend_back(queries, kv, lengths, first, logs, grad):
    b, t, width = queries.shape
    hd = kv.shape[2] // 2
    scale = hd**-0.5
    dqs, dkvs = [], []
    for s in range(b):
        keys, values = kv[s, :, :hd], kv[s, :, hd:]
        allowed = pairs_allowed(first, t, kv.shape[1], lengths[s])
        dk = dv = 0.0
        dq = []
        for h in range(width // hd):
            q = queries[s, :, h * hd : (h + 1) * hd]
            g = grad[s, :, h * hd : (h + 1) * hd]
            scores = jnp.where(allowed, mm(q, keys, 1, 1) * scale, -jnp.inf)
            p = jnp.exp(scores - logs[s, :, h : h + 1])
            dp = mm(g, values, 1, 1)
            ds = (p * (dp - jnp.sum(p * dp, axis=1, keepdims=True))).astype(BF)
            dq.append((mm(ds, keys, 1, 0) * scale).astype(BF))
            dk = dk + mm(ds, q, 0, 0) * scale
            dv = dv + mm(p.astype(BF), g, 0, 0)
        dqs.append(jnp.concatenate(dq, axis=1))
        dkvs.append(jnp.concatenate([dk, dv], axis=1).astype(BF))
    return jnp.stack(dqs), jnp.stack(dkvs)


def local(
    tokens,
    lengths,
    cotangent,
    norm1_gain,
    norm1_bias,
    query_weight,
    kv_weight,
    out_weight,
    norm2_gain,
    norm2_bias,
    up_weight,
    down_weight,
):
    b, t, f = tokens.shape
    nd, nr, nc = (lax.axis_size(a) for a in ("dp", "row", "col"))
    dp, row, col = (lax.axis_index(a) for a in ("dp", "row", "col"))
    m, d = b * t, f * nc
    own = m // nc
    hd = kv_weight.shape[1] // 2
    plane = ("dp", "col")

    slot = row * t + jnp.arange(t, dtype=jnp.int32)
    keep = (slot[None, :] < lengths[:, None]).astype(F32).reshape(m, 1)

    def mine(x):
        return lax.dynamic_slice_in_dim(x, col * own, own, 0)

    def half(w):
        n = w.shape[0] // nd
        return lax.dynamic_slice_in_dim(w, dp * n, n, 0)

    wq = gather(turn(query_weight.T), "row")
    wo = gather(turn(out_weight), "row")
    wu = gather(turn(half(up_weight.T)), "row")
    wd = gather(turn(half(down_weight)), "row")
    wkv = gather(kv_weight, "col")
    vectors = gather(jnp.stack([norm1_gain, norm1_bias, norm2_gain, norm2_bias]), "col", 1)
    gain1, bias1, gain2, bias2 = (vectors[i : i + 1] for i in range(4))

    x = gather(tokens.reshape(m, f), "col", 1)
    grad_final = (keep * cotangent.reshape(m, f).astype(F32)).astype(BF)
    grad_own = turn(grad_final)
    grad_all = gather(grad_own, plane)

    keep_own = mine(keep)
    centre, inverse = norm_stats(x.astype(F32))
    one = norm_apply(x.astype(F32), centre, inverse, gain1, bias1, keep)
    one_own = mine(one)
    queries = mm(one, wq, 1, 1).astype(BF).reshape(b, t, -1)
    kv_own = mm(one_own, wkv, 1, 0).astype(BF)
    kv = gather(kv_own, ("row", "col")).reshape(nr, b, t, 2 * hd)
    kv = kv.transpose(1, 0, 2, 3).reshape(b, nr * t, 2 * hd)
    attended, logs = attend(queries, kv, lengths, row * t)
    attended = attended.reshape(m, -1)
    x_own = mine(x).astype(F32)
    middle = x_own + scatter(mm(attended, wo, 1, 0).astype(BF), "col").astype(F32)

    centre2, inverse2 = norm_stats(middle)
    two_own = norm_apply(middle, centre2, inverse2, gain2, bias2, keep_own)
    two = gather(two_own, plane)
    sums = mm(two, wu, 1, 1)
    activated, pull = jax.vjp(lambda v: jax.nn.gelu(v, approximate=True), sums)
    activated = activated.astype(BF)
    ffn = scatter(mm(activated, wd, 1, 0).astype(BF), plane)
    out = turn_back((keep_own * (middle + ffn.astype(F32))).astype(BF))

    grad_act = mm(grad_all, wd, 1, 1)
    grad_up = pull(grad_act)[0].astype(BF)
    d_down = scatter(mm(activated, grad_all, 0, 0).astype(BF), "row")
    d_up = scatter(mm(grad_up, two, 0, 0).astype(BF), "row")
    e_two = scatter(mm(grad_up, wu, 1, 0).astype(BF), plane).astype(F32)
    normed2 = (middle - centre2) * inverse2
    back_two, g_gain2, g_bias2 = norm_backward(e_two, normed2, inverse2, gain2, keep_own)
    grad_middle = grad_own.astype(F32) + back_two

    grad_attn = gather(grad_middle.astype(BF), "col")
    grad_att = mm(grad_attn, wo, 1, 1).astype(BF)
    d_out = scatter(mm(attended, grad_attn, 0, 0).astype(BF), "row")
    dq, dkv = attend_back(queries, kv, lengths, row * t, logs, grad_att.reshape(b, t, -1))
    dq = dq.reshape(m, -1)
    dkv = dkv.reshape(b, nr, t, 2 * hd).transpose(1, 0, 2, 3).reshape(nr * m, 2 * hd)
    dkv_own = scatter(dkv, ("row", "col"))
    d_query = scatter(mm(dq, one, 0, 0).astype(BF), "row")
    e_one = scatter(mm(dq, wq, 1, 0).astype(BF), "col").astype(F32) + mm(dkv_own, wkv, 1, 1)
    normed1 = (x_own - mine(centre)) * mine(inverse)
    back_one, g_gain1, g_bias1 = norm_backward(e_one, normed1, mine(inverse), gain1, keep_own)
    grad_in = turn_back((grad_middle + back_one).astype(BF))

    d_kv = scatter(mm(one_own, dkv_own, 0, 0).astype(BF), "col")
    d_kv = lax.psum(d_kv, ("dp", "row")).astype(F32)
    small = lax.psum(jnp.stack([g_gain1, g_bias1, g_gain2, g_bias2]), ("dp", "row", "col"))
    small = lax.dynamic_slice_in_dim(small, col * f, f, 1)
    d_query = lax.psum(turn_back(d_query), "dp").astype(F32).T
    d_out = lax.psum(turn_back(d_out), "dp").astype(F32)
    d_up = gather(turn_back(d_up), "dp").astype(F32).T
    d_down = gather(turn_back(d_down), "dp").astype(F32)
    return (
        out.reshape(b, t, f),
        grad_in.reshape(b, t, f),
        small[0],
        small[1],
        d_query,
        d_kv,
        d_out,
        small[2],
        small[3],
        d_up,
        d_down,
    )


def solution(mesh):
    act, vec = P("dp", "row", "col"), P("col")
    wide, tall = P("col", "row"), P("row", "col")
    return jax.shard_map(
        local,
        mesh=mesh,
        in_specs=(act, P("dp"), act, vec, vec, wide, P("col", None), tall, vec, vec, wide, tall),
        out_specs=(act, act, vec, vec, wide, P("col", None), tall, vec, vec, wide, tall),
        check_vma=False,
    )
```
